32 devices in a mesh: tm: 2 (over x), gx: 4 (over z), gy: 4 (over y, core).
Axes of the slice: x: 2, y: 2, z: 4, core: 2. Of those that a mesh axis runs over, the one named last changes fastest.
Arguments:
- initial: float32 [64, 16, 8, 128], P(None, 'gx', 'gy'), may hold values from -6 to 6
- source: float32 [64, 16, 8, 128], P(None, 'gx', 'gy'), may hold values from -1.5 to 1.5
- self_block: float32 [64, 64], replicated, may hold values from -1.01 to 0.01
- face_blocks: float32 [6, 64, 64], replicated, may hold values from -0.35 to 0.35
- coarse_block: float32 [64, 64], replicated, may hold values from -0.01 to 0.92
- face_code: int32 [16, 8, 128], P('gx', 'gy'), may hold values from 0 to 63
- step_counts: int32 [8], P('tm'), may hold values from 2 to 3, as said below
Outputs:
- final_states: float32 [8, 64, 16, 8, 128], P('tm', None, 'gx', 'gy')
The draws below stay inside these ranges and needn't reach their ends.
Inputs may be any that keep to these rules, and one draw needn't show every extreme that they name: `step_counts`: some slice has exactly 3 steps in every draw.
All inputs are finite; a program needn't handle non-finite values.
Results may differ from the reference program's by a relative error of at most 0.0003.
Values sent between devices are 32-bit elements; how exact they have to be, the bound alone decides.
A program may use at most 128 MiB of HBM per device.

```python
import math
import jax
import jax.numpy as jnp
from jax import lax

DOF = 64
EZ = 128
MAXSTEP = 3
ITERS = 2
SLICES = 8
NXE = 16
NYE = 8


def decay_rates(key):
    logs = jax.random.uniform(jax.random.fold_in(key, 11), (DOF,), jnp.float32, math.log(0.1), 0.0)
    return jnp.exp(logs)


def draw_self_block(key, part):
    rates = decay_rates(key)
    noise_key = jax.random.fold_in(key, 21)
    noise = jnp.clip(jax.random.normal(noise_key, (DOF, DOF), jnp.float32) * 0.002, -0.008, 0.008)
    return noise - jnp.diag(rates)


def draw_coarse_block(key, part):
    rates = decay_rates(key)
    noise_key = jax.random.fold_in(key, 31)
    noise = jnp.clip(jax.random.normal(noise_key, (DOF, DOF), jnp.float32) * 0.002, -0.008, 0.008)
    return noise + jnp.diag(jnp.exp(-rates))


def draw_face_blocks(key, part):
    blocks = []
    for pair in range(3):
        pair_key = jax.random.fold_in(key, 41 + pair)
        lower = jnp.clip(jax.random.normal(pair_key, (DOF, DOF), jnp.float32) * 0.1, -0.35, 0.35)
        blocks.append(lower)
        blocks.append(-jnp.transpose(lower))
    return jnp.stack(blocks)


def draw_step_counts(key, part):
    key_heavy, key_spot = jax.random.split(key, 2)
    heavy = jax.random.randint(key_heavy, (SLICES,), 0, 4) == 0
    counts = jnp.where(heavy, MAXSTEP, 2)
    spot = jax.random.randint(key_spot, (), 0, SLICES)
    counts = jnp.where(jnp.arange(SLICES) == spot, MAXSTEP, counts)
    return counts.astype(jnp.int32)


def plant(values, stream_key, low, top_value):
    spot = [jax.random.randint(jax.random.fold_in(stream_key, axis), (), 0, length) for axis, length in enumerate(values.shape)]
    longest = values.shape.index(max(values.shape))
    next_to = spot[:longest] + [(spot[longest] + 1) % values.shape[longest]] + spot[longest + 1:]
    return values.at[tuple(spot)].set(low).at[tuple(next_to)].set(top_value)


def steps_of(rng, shape, shards, least, top_value):
    gain, own = 1.0, jax.random.fold_in(rng, 6)
    for dim, parts in shards:
        steps = jnp.exp(jax.random.uniform(jax.random.fold_in(own, dim), (parts,), jnp.float32, least / len(shards), top_value / len(shards)))
        gain = gain * jnp.repeat(steps, shape[dim] // parts).reshape([-1 if axis == dim else 1 for axis in range(len(shape))])
    return gain


def gaussian(rng, shape, scale, most, pieces=(), kind=jnp.bfloat16):
    drawn = jax.random.normal(rng, shape, jnp.float32) * scale
    if len(pieces) > 0:
        drawn = steps_of(rng, shape, pieces, -0.22, 0.18) * drawn
    return jnp.clip(drawn, min=-most, max=most).astype(kind)


def setup_inputs(seed: int = 0) -> dict:
    key_of = jax.random.split(jax.random.key(seed), 8)
    initial = gaussian(key_of[0], (DOF, NXE, NYE, EZ), 1.0, 6.0, ((1, 4), (2, 4)), jnp.float32)
    source = gaussian(key_of[1], (DOF, NXE, NYE, EZ), 0.25, 1.5, ((1, 4), (2, 4)), jnp.float32)
    self_block = draw_self_block(jax.random.fold_in(key_of[7], 71), 0)
    face_blocks = draw_face_blocks(jax.random.fold_in(key_of[7], 71), 0)
    coarse_block = draw_coarse_block(jax.random.fold_in(key_of[7], 71), 0)
    face_code = plant(jax.random.randint(key_of[5], (NXE, NYE, EZ), 0, 64), jax.random.fold_in(key_of[5], 1), 0, 63).astype(jnp.int32)
    step_counts = draw_step_counts(jax.random.fold_in(key_of[7], 71), 0)
    return dict(initial=initial, source=source, self_block=self_block, face_blocks=face_blocks, coarse_block=coarse_block, face_code=face_code, step_counts=step_counts)


HIGHEST = lax.Precision.HIGHEST


def blockwise(matrix, values):
    return jnp.einsum("ij,jxyz->ixyz", matrix, values, precision=HIGHEST)


def face_masks(face_code):
    powers = (2 ** jnp.arange(6)).astype(jnp.int32)
    return ((face_code[None] // powers[:, None, None, None]) % 2).astype(jnp.float32)


def operate(current, self_block, face_blocks, open_faces):
    zero_plane = jnp.zeros_like(current[:, :, :, :1])
    below_plane = jnp.concatenate([zero_plane, current[:, :, :, :-1]], axis=3)
    above_plane = jnp.concatenate([current[:, :, :, 1:], zero_plane], axis=3)
    neighbours = [jnp.roll(current, 1, axis=1), jnp.roll(current, -1, axis=1),
                  jnp.roll(current, 1, axis=2), jnp.roll(current, -1, axis=2),
                  below_plane, above_plane]
    accumulated = blockwise(self_block, current)
    for facing in range(6):
        accumulated = accumulated + open_faces[facing] * blockwise(face_blocks[facing], neighbours[facing])
    return accumulated


def sweep(initial, coarse_block, corrections):
    def stepper(current, correction):
        following = blockwise(coarse_block, current) + correction
        return following, (current, following)
    unused, (starts, finish_states) = lax.scan(stepper, initial, corrections)
    return starts, finish_states


def reference(initial, source, self_block, face_blocks, coarse_block, face_code, step_counts):
    open_faces = face_masks(face_code)

    def propagate(packed):
        beginning, step_total = packed
        step_size = 1.0 / step_total.astype(jnp.float32)

        def advance(number, current):
            slope_one = operate(current, self_block, face_blocks, open_faces) + source
            middle = current + step_size * slope_one
            slope_two = operate(middle, self_block, face_blocks, open_faces) + source
            moved = current + (0.5 * step_size) * (slope_one + slope_two)
            return jnp.where(number < step_total, moved, current)
        return lax.fori_loop(0, MAXSTEP, advance, beginning)

    corrections = jnp.broadcast_to(source, (SLICES,) + source.shape)
    starts, finish_states = sweep(initial, coarse_block, corrections)
    for iteration in range(ITERS):
        finals = lax.map(propagate, (starts, step_counts))
        coarse_part = jnp.einsum("ij,sjxyz->sixyz", coarse_block, starts, precision=HIGHEST)
        corrections = finals - coarse_part
        starts, finish_states = sweep(initial, coarse_block, corrections)
    return finish_states
```

```python
import functools

import jax
import jax.numpy as jnp
from jax import lax
from jax.experimental import pallas as pl
from jax.experimental.pallas import tpu as pltpu
from jax.sharding import PartitionSpec as P

MAXSTEP = 3
ITERS = 2
MESH = pl.DeviceIdType.MESH


def split3(v):
    high = v.astype(jnp.bfloat16)
    low = (v - high.astype(jnp.float32)).astype(jnp.bfloat16)
    return jnp.concatenate([high, low, high], axis=0)


def split3_weights(w):
    high = w.astype(jnp.bfloat16)
    low = (w - high.astype(jnp.float32)).astype(jnp.bfloat16)
    return jnp.concatenate([high, high, low], axis=1)


def mul(w, v3):
    return jnp.dot(w, v3, preferred_element_type=jnp.float32)


def kernel(nt, nx, ny, mine, weights, step_ref, gain_ref, out,
           field, wide, prod, cur, mid, slope, corr, recv, local, starts, halo, arrived, powers, mixer,
           gsend, grecv, hsend, hrecv, asend, arecv, bsend, brecv, tsend, trecv):
    tm, gx, gy = lax.axis_index("tm"), lax.axis_index("gx"), lax.axis_index("gy")
    right, left = lax.rem(gx + 1, nx), lax.rem(gx + nx - 1, nx)
    later, earlier = lax.rem(tm + 1, nt), lax.rem(tm + nt - 1, nt)
    peers = [lax.rem(gy + d, ny) for d in range(1, ny)]
    xs = mine.shape[0]
    dof = weights.shape[1]

    barrier = pltpu.get_barrier_semaphore()
    for target in [{"gx": left}, {"gx": right}, {"tm": later}, {"tm": earlier}] + [{"gy": p} for p in peers]:
        pl.semaphore_signal(barrier, inc=1, device_id=target, device_id_type=MESH)
    pl.semaphore_wait(barrier, 4 + len(peers))

    def exchange(source_of, target, send, receive):
        copies = []
        for d, peer in enumerate(peers):
            copy = pltpu.make_async_remote_copy(
                src_ref=source_of(peer), dst_ref=target, send_sem=send.at[d], recv_sem=receive.at[d],
                device_id={"gy": peer}, device_id_type=MESH)
            copy.start()
            copies.append(copy)
        return copies

    copies = exchange(lambda peer: mine, field.at[:, gy], gsend, grecv)

    wide[...] = split3_weights(weights[...])
    coarse = wide[7 * dof:8 * dof, :]
    power = weights[7 * dof:8 * dof, :]
    for j in range(ny):
        powers[j * dof:(j + 1) * dof, :] = split3_weights(power)
        power = mul(coarse, split3(power)) if j < ny - 1 else power
    rows = lax.broadcasted_iota(jnp.int32, (dof, dof), 0)
    cols = lax.broadcasted_iota(jnp.int32, (dof, dof), 1)
    identity = (rows == cols).astype(jnp.float32)

    def raise_power(_, pair):
        high, total = pair
        return mul(coarse, split3(high)), mul(coarse, split3(total)) + identity

    high, total = lax.fori_loop(0, tm * ny + gy, raise_power, (identity, jnp.zeros_like(identity)))
    mixer[...] = jnp.concatenate([split3_weights(high), split3_weights(total)], axis=1)
    for x in range(xs):
        field[x, gy] = mine[x]
    for copy in copies:
        copy.wait()

    def first_starts(x, _):
        for y in range(ny):
            cur[x, y] = mul(mixer[...], jnp.concatenate(
                [split3(field[x, y, 0:dof, :]), split3(field[x, y, dof:2 * dof, :])], axis=0))
        return 0

    lax.fori_loop(0, xs, first_starts, 0)

    step = step_ref[gy]

    def combine(x, y):
        here = prod.at[x + 1, y]

        def mask(f):
            return field[x, y, 2 * dof + f:2 * dof + f + 1, :]

        lower, upper = prod.at[x + 1, (y + ny - 1) % ny], prod.at[x + 1, (y + 1) % ny]

        def face(f):
            return slice((f + 1) * dof, (f + 2) * dof)

        before = jnp.concatenate([lower[face(2), 128:], here[face(2), :128]], axis=1)
        after = jnp.concatenate([here[face(3), 128:], upper[face(3), :128]], axis=1)
        below = jnp.concatenate([pltpu.roll(here[face(4), :128], 1, 1), pltpu.roll(here[face(4), 128:], 1, 1)], axis=1)
        above = jnp.concatenate([pltpu.roll(here[face(5), :128], 127, 1), pltpu.roll(here[face(5), 128:], 127, 1)], axis=1)
        total = here[0:dof, :] + field[x, y, dof:2 * dof, :]
        total = total + mask(0) * prod[x, y, face(0), :]
        total = total + mask(1) * prod[x + 2, y, face(1), :]
        total = total + mask(2) * before
        total = total + mask(3) * after
        total = total + mask(4) * below
        return total + mask(5) * above

    def stage(second, finish):
        source = mid if second else cur
        slot = 1 if second else 0
        to_left = pltpu.make_async_remote_copy(
            src_ref=source.at[0], dst_ref=halo.at[slot, 1], send_sem=hsend.at[slot, 0], recv_sem=hrecv.at[slot, 1],
            device_id={"gx": left}, device_id_type=MESH)
        to_right = pltpu.make_async_remote_copy(
            src_ref=source.at[xs - 1], dst_ref=halo.at[slot, 0], send_sem=hsend.at[slot, 1], recv_sem=hrecv.at[slot, 0],
            device_id={"gx": right}, device_id_type=MESH)
        to_left.start()
        to_right.start()

        def products(x, _):
            for y in range(ny):
                prod[x + 1, y] = mul(wide[...], split3(source[x, y]))
            return 0

        lax.fori_loop(0, xs, products, 0)

        def inner(x, _):
            for y in range(ny):
                finish(x, y, combine(x, y))
            return 0

        lax.fori_loop(1, xs - 1, inner, 0)
        to_left.wait()
        to_right.wait()
        for y in range(ny):
            prod[0, y, dof:2 * dof, :] = mul(wide[dof:2 * dof, :], split3(halo[slot, 0, y]))
            prod[xs + 1, y, 2 * dof:3 * dof, :] = mul(wide[2 * dof:3 * dof, :], split3(halo[slot, 1, y]))
        for x in (0, xs - 1):
            for y in range(ny):
                finish(x, y, combine(x, y))

    def advance(number, _):
        gain = gain_ref[number, gy]

        def to_middle(x, y, rate):
            slope[x, y] = rate
            mid[x, y] = cur[x, y] + step * rate

        def to_next(x, y, rate):
            cur[x, y] = cur[x, y] + gain * (slope[x, y] + rate)

        stage(False, to_middle)
        stage(True, to_next)
        return 0

    for iteration in range(ITERS):
        def keep_coarse(x, _):
            for y in range(ny):
                corr[x, y] = mul(coarse, split3(cur[x, y]))
            return 0

        lax.fori_loop(0, xs, keep_coarse, 0)
        lax.fori_loop(0, MAXSTEP, advance, 0)

        def correct(x, _):
            for y in range(ny):
                corr[x, y] = cur[x, y] - corr[x, y]
            return 0

        lax.fori_loop(0, xs, correct, 0)
        copies = exchange(lambda peer: corr.at[:, peer], recv.at[gy], asend, arecv)
        for x in range(xs):
            recv[gy, x] = corr[x, gy]
        for copy in copies:
            copy.wait()

        def run_local(x, _):
            now = recv[0, x]
            local[0, x] = now
            for j in range(1, ny):
                now = mul(coarse, split3(now)) + recv[j, x]
                local[j, x] = now
            return 0

        lax.fori_loop(0, xs, run_local, 0)
        for x in range(xs):
            starts[0, x] = mine[x, 0:dof, :]
        for relay in range(nt - 1):
            at = iteration * (nt - 1) + relay
            for x in range(xs):
                starts[ny, x] = mul(powers[(ny - 1) * dof:, :], split3(starts[0, x])) + local[ny - 1, x]
            copy = pltpu.make_async_remote_copy(
                src_ref=starts.at[ny], dst_ref=arrived.at[at], send_sem=tsend.at[at], recv_sem=trecv.at[at],
                device_id={"tm": later}, device_id_type=MESH)
            copy.start()
            copy.wait()
            for x in range(xs):
                starts[0, x] = jnp.where(tm == 0, mine[x, 0:dof, :], arrived[at, x])
        last = iteration == ITERS - 1

        def finish_all(x, _):
            shares = mul(powers[...], split3(starts[0, x]))
            for j in range(ny):
                ended = shares[j * dof:(j + 1) * dof, :] + local[j, x]
                if last:
                    out[j, x] = ended
                elif j < ny - 1:
                    starts[j + 1, x] = ended
            return 0

        lax.fori_loop(0, xs, finish_all, 0)
        if not last:
            copies = exchange(lambda peer: starts.at[peer], cur.at[:, gy], bsend, brecv)
            for x in range(xs):
                cur[x, gy] = starts[gy, x]
            for copy in copies:
                copy.wait()


def per_device(nt, nx, ny, initial, source, self_block, face_blocks, coarse_block, face_code, step_counts):
    dof, xs, ys, ez = initial.shape
    assert step_counts.shape[0] == ny
    width = ys * ez
    depth = jnp.arange(ez)
    powers = (2 ** jnp.arange(6)).astype(jnp.int32)
    faces = (face_code[:, None] // powers[None, :, None, None] % 2).astype(jnp.float32)
    inside = jnp.ones((6, ez), jnp.float32).at[4].set((depth > 0) * 1.0).at[5].set((depth < ez - 1) * 1.0)
    faces = faces * inside[None, :, None, :]
    faces = jnp.pad(faces, ((0, 0), (0, 2), (0, 0), (0, 0))).reshape(xs, 8, width)

    def chunked(v):
        return v.transpose(1, 0, 2, 3).reshape(xs, dof, width)

    mine = jnp.concatenate([chunked(initial), chunked(source), faces], axis=1)
    weights = jnp.concatenate([self_block[None], face_blocks, coarse_block[None]], axis=0).reshape(8 * dof, dof)
    step = 1.0 / step_counts.astype(jnp.float32)
    gain = jnp.where(jnp.arange(MAXSTEP)[:, None] < step_counts[None, :], 0.5 * step[None, :], 0.0)
    f32, bf16 = jnp.float32, jnp.bfloat16
    tall = 2 * dof + 8
    slabs = (xs, ny, dof, width)
    dma = pltpu.SemaphoreType.DMA
    result = pl.pallas_call(
        functools.partial(kernel, nt, nx, ny),
        out_shape=jax.ShapeDtypeStruct((ny, xs, dof, width), f32),
        in_specs=[pl.BlockSpec(memory_space=pltpu.VMEM)] * 2 + [pl.BlockSpec(memory_space=pltpu.SMEM)] * 2,
        out_specs=pl.BlockSpec(memory_space=pltpu.VMEM),
        scratch_shapes=[
            pltpu.VMEM((xs, ny, tall, width), f32),
            pltpu.VMEM((8 * dof, 3 * dof), bf16),
            pltpu.VMEM((xs + 2, ny, 8 * dof, width), f32),
            pltpu.VMEM(slabs, f32),
            pltpu.VMEM(slabs, f32),
            pltpu.VMEM(slabs, f32),
            pltpu.VMEM(slabs, f32),
            pltpu.VMEM((ny, xs, dof, width), f32),
            pltpu.VMEM((ny, xs, dof, width), f32),
            pltpu.VMEM((ny + 1, xs, dof, width), f32),
            pltpu.VMEM((2, 2, ny, dof, width), f32),
            pltpu.VMEM((max(1, ITERS * (nt - 1)), xs, dof, width), f32),
            pltpu.VMEM((ny * dof, 3 * dof), bf16),
            pltpu.VMEM((dof, 6 * dof), bf16),
            dma((ny - 1,)), dma((ny - 1,)),
            dma((2, 2)), dma((2, 2)),
            dma((ny - 1,)), dma((ny - 1,)),
            dma((ny - 1,)), dma((ny - 1,)),
            dma((max(1, ITERS * (nt - 1)),)), dma((max(1, ITERS * (nt - 1)),)),
        ],
        compiler_params=pltpu.CompilerParams(collective_id=0, has_side_effects=True, vmem_limit_bytes=50 << 20),
    )(mine, weights, step, gain)
    return result.reshape(ny, xs, dof, ys, ez).transpose(0, 2, 1, 3, 4)


def solution(mesh):
    nt, nx, ny = (mesh.shape[name] for name in ("tm", "gx", "gy"))
    return jax.shard_map(
        functools.partial(per_device, nt, nx, ny),
        mesh=mesh,
        in_specs=(
            P(None, "gx", "gy", None),
            P(None, "gx", "gy", None),
            P(),
            P(),
            P(),
            P("gx", "gy", None),
            P("tm"),
        ),
        out_specs=P("tm", None, "gx", "gy", None),
        check_vma=False,
    )
```

```python
import functools

import jax
import jax.numpy as jnp
from jax import lax
from jax.experimental import pallas as pl
from jax.experimental.pallas import tpu as pltpu
from jax.sharding import PartitionSpec as P

MAXSTEP = 3
ITERS = 2
MESH = pl.DeviceIdType.MESH


def split3(v):
    high = v.astype(jnp.bfloat16)
    low = (v - high.astype(jnp.float32)).astype(jnp.bfloat16)
    return jnp.concatenate([high, low, high], axis=0)


def split3_weights(w):
    high = w.astype(jnp.bfloat16)
    low = (w - high.astype(jnp.float32)).astype(jnp.bfloat16)
    return jnp.concatenate([high, high, low], axis=1)


def mul(w, v3):
    return jnp.dot(w, v3, preferred_element_type=jnp.float32)


def kernel(nt, nx, ny, mine, weights, step_ref, gain_ref, out,
           field, wide, prod, cur, mid, slope, corr, recv, local, starts, halo, arrived, powers, mixer,
           gsend, grecv, hsend, hrecv, asend, arecv, bsend, brecv, tsend, trecv):
    tm, gx, gy = lax.axis_index("tm"), lax.axis_index("gx"), lax.axis_index("gy")
    right, left = lax.rem(gx + 1, nx), lax.rem(gx + nx - 1, nx)
    later, earlier = lax.rem(tm + 1, nt), lax.rem(tm + nt - 1, nt)
    peers = [lax.rem(gy + d, ny) for d in range(1, ny)]
    behind = [lax.rem(gy + ny - d, ny) for d in range(1, ny)]
    sibling = gy + 1 - 2 * lax.rem(gy, 2)
    across = ny - 1 - gy
    xs = mine.shape[0]
    dof = weights.shape[1]
    edges, inside = [0, xs - 1], list(range(1, xs - 1))

    barrier = pltpu.get_barrier_semaphore()
    for target in [{"gx": left}, {"gx": right}, {"tm": later}, {"tm": earlier}] + [{"gy": p} for p in peers]:
        pl.semaphore_signal(barrier, inc=1, device_id=target, device_id_type=MESH)
    pl.semaphore_wait(barrier, 4 + len(peers))

    def remote(source, target, send, receive, device):
        return pltpu.make_async_remote_copy(src_ref=source, dst_ref=target, send_sem=send, recv_sem=receive,
                                            device_id=device, device_id_type=MESH)

    def halo_copies(slot, y):
        source = mid if slot == 1 else cur
        return [
            remote(source.at[0, y], halo.at[slot, 1, y], hsend.at[slot, 0, y], hrecv.at[slot, 1, y], {"gx": left}),
            remote(source.at[xs - 1, y], halo.at[slot, 0, y], hsend.at[slot, 1, y], hrecv.at[slot, 0, y], {"gx": right}),
        ]

    def send_halo(slot, y):
        for copy in halo_copies(slot, y):
            copy.start()

    crossing, passing, onward = {}, {}, {}
    for x in edges + inside:
        crossing[x] = remote(mine.at[x], field.at[x, gy], gsend.at[0, x], grecv.at[0, x], {"gy": across})
        passing[x] = remote(mine.at[x], field.at[x, gy], gsend.at[1, x], grecv.at[1, x], {"gy": sibling})
        onward[x] = remote(field.at[x, across], field.at[x, across], gsend.at[2, x], grecv.at[2, x], {"gy": sibling})
        crossing[x].start()
        passing[x].start()

    wide[...] = split3_weights(weights[...])
    coarse = wide[7 * dof:8 * dof, :]
    power = weights[7 * dof:8 * dof, :]
    for j in range(ny):
        powers[j * dof:(j + 1) * dof, :] = split3_weights(power)
        power = mul(coarse, split3(power)) if j < ny - 1 else power
    rows = lax.broadcasted_iota(jnp.int32, (dof, dof), 0)
    cols = lax.broadcasted_iota(jnp.int32, (dof, dof), 1)
    identity = (rows == cols).astype(jnp.float32)

    def raise_power(_, pair):
        high, total = pair
        return mul(coarse, split3(high)), mul(coarse, split3(total)) + identity

    high, total = lax.fori_loop(0, tm * ny + gy, raise_power, (identity, jnp.zeros_like(identity)))
    mixer[...] = jnp.concatenate([split3_weights(high), split3_weights(total)], axis=1)
    for x in edges + inside:
        field[x, gy] = mine[x]
        crossing[x].wait()
        onward[x].start()
        passing[x].wait()
        onward[x].wait()
        for y in range(ny):
            cur[x, y] = mul(mixer[...], jnp.concatenate(
                [split3(field[x, y, 0:dof, :]), split3(field[x, y, dof:2 * dof, :])], axis=0))
        if x == edges[-1]:
            for y in range(ny):
                send_halo(0, y)

    step = step_ref[gy]

    def combine(x, y):
        here = prod.at[x + 1, y]

        def mask(f):
            return field[x, y, 2 * dof + f:2 * dof + f + 1, :]

        lower, upper = prod.at[x + 1, (y + ny - 1) % ny], prod.at[x + 1, (y + 1) % ny]

        def face(f):
            return slice((f + 1) * dof, (f + 2) * dof)

        before = jnp.concatenate([lower[face(2), 128:], here[face(2), :128]], axis=1)
        after = jnp.concatenate([here[face(3), 128:], upper[face(3), :128]], axis=1)
        below = jnp.concatenate([pltpu.roll(here[face(4), :128], 1, 1), pltpu.roll(here[face(4), 128:], 1, 1)], axis=1)
        above = jnp.concatenate([pltpu.roll(here[face(5), :128], 127, 1), pltpu.roll(here[face(5), 128:], 127, 1)], axis=1)
        total = here[0:dof, :] + field[x, y, dof:2 * dof, :]
        total = total + mask(0) * prod[x, y, face(0), :]
        total = total + mask(1) * prod[x + 2, y, face(1), :]
        total = total + mask(2) * before
        total = total + mask(3) * after
        total = total + mask(4) * below
        return total + mask(5) * above

    def stage(slot, finish, after_inside, after_edge):
        source = mid if slot == 1 else cur

        def products(x, _):
            for y in range(ny):
                prod[x + 1, y] = mul(wide[...], split3(source[x, y]))
            return 0

        lax.fori_loop(0, xs, products, 0)

        def inner(x, _):
            for y in range(ny):
                finish(x, y, combine(x, y))
            return 0

        lax.fori_loop(1, xs - 1, inner, 0)
        after_inside()
        for y in range(ny):
            for copy in halo_copies(slot, y):
                copy.wait()
            prod[0, y, dof:2 * dof, :] = mul(wide[dof:2 * dof, :], split3(halo[slot, 0, y]))
            prod[xs + 1, y, 2 * dof:3 * dof, :] = mul(wide[2 * dof:3 * dof, :], split3(halo[slot, 1, y]))
            for x in edges:
                finish(x, y, combine(x, y))
            after_edge(y)

    def nothing(*_):
        return None

    def to_middle(x, y, rate):
        slope[x, y] = rate
        mid[x, y] = cur[x, y] + step * rate

    def advance(number, _):
        gain = gain_ref[number, gy]

        def to_next(x, y, rate):
            cur[x, y] = cur[x, y] + gain * (slope[x, y] + rate)

        stage(0, to_middle, nothing, functools.partial(send_halo, 1))
        stage(1, to_next, nothing, functools.partial(send_halo, 0))
        return 0

    def incoming(at, x):
        return jnp.where(tm == 0, mine[x, 0:dof, :], arrived[at, x])

    for iteration in range(ITERS):
        last = iteration == ITERS - 1

        def keep_coarse(x, _):
            for y in range(ny):
                corr[x, y] = mul(coarse, split3(cur[x, y]))
            return 0

        lax.fori_loop(0, xs, keep_coarse, 0)
        lax.fori_loop(0, MAXSTEP - 1, advance, 0)
        gain = gain_ref[MAXSTEP - 1, gy]
        giving = {}

        def to_correction(x, y, rate):
            corr[x, y] = cur[x, y] + gain * (slope[x, y] + rate) - corr[x, y]

        def give(places):
            for x in places:
                for d, peer in enumerate(peers):
                    giving[x, d] = remote(corr.at[x, peer], recv.at[gy, x], asend.at[x, d], arecv.at[x, d], {"gy": peer})
                    giving[x, d].start()

        stage(0, to_middle, nothing, functools.partial(send_halo, 1))
        stage(1, to_correction, functools.partial(give, inside), nothing)
        give(edges)

        relays = {}

        def relay(number, x, entering):
            at = iteration * (nt - 1) + number
            starts[ny, x] = mul(powers[(ny - 1) * dof:, :], split3(entering)) + local[ny - 1, x]
            relays[x] = remote(starts.at[ny, x], arrived.at[at, x], tsend.at[at, x], trecv.at[at, x], {"tm": later})
            relays[x].start()

        for x in inside + edges:
            recv[gy, x] = corr[x, gy]
            for d in range(len(peers)):
                giving[x, d].wait()
            now = recv[0, x]
            local[0, x] = now
            for j in range(1, ny):
                now = mul(coarse, split3(now)) + recv[j, x]
                local[j, x] = now
            if nt > 1:
                relay(0, x, mine[x, 0:dof, :])
        for number in range(1, nt - 1):
            for x in inside + edges:
                relays[x].wait()
                relay(number, x, incoming(iteration * (nt - 1) + number - 1, x))
        taking = {}
        for x in inside + edges:
            if nt > 1:
                relays[x].wait()
                starts[0, x] = incoming(iteration * (nt - 1) + nt - 2, x)
            else:
                starts[0, x] = mine[x, 0:dof, :]
            shares = mul(powers[...], split3(starts[0, x]))
            for j in range(ny):
                ended = shares[j * dof:(j + 1) * dof, :] + local[j, x]
                if last:
                    out[j, x] = ended
                elif j < ny - 1:
                    starts[j + 1, x] = ended
            if not last:
                cur[x, gy] = starts[gy, x]
                for d, peer in enumerate(peers):
                    taking[x, d] = remote(starts.at[peer, x], cur.at[x, gy], bsend.at[x, d], brecv.at[x, d], {"gy": peer})
                    taking[x, d].start()
        if not last:
            send_halo(0, gy)
            for d in range(len(peers)):
                for x in edges:
                    taking[x, d].wait()
                send_halo(0, behind[d])
            for x in inside:
                for d in range(len(peers)):
                    taking[x, d].wait()


def per_device(nt, nx, ny, initial, source, self_block, face_blocks, coarse_block, face_code, step_counts):
    dof, xs, ys, ez = initial.shape
    assert step_counts.shape[0] == ny == 4
    width = ys * ez
    depth = jnp.arange(ez)
    powers = (2 ** jnp.arange(6)).astype(jnp.int32)
    faces = (face_code[:, None] // powers[None, :, None, None] % 2).astype(jnp.float32)
    inside = jnp.ones((6, ez), jnp.float32).at[4].set((depth > 0) * 1.0).at[5].set((depth < ez - 1) * 1.0)
    faces = faces * inside[None, :, None, :]
    faces = jnp.pad(faces, ((0, 0), (0, 2), (0, 0), (0, 0))).reshape(xs, 8, width)

    def chunked(v):
        return v.transpose(1, 0, 2, 3).reshape(xs, dof, width)

    mine = jnp.concatenate([chunked(initial), chunked(source), faces], axis=1)
    weights = jnp.concatenate([self_block[None], face_blocks, coarse_block[None]], axis=0).reshape(8 * dof, dof)
    step = 1.0 / step_counts.astype(jnp.float32)
    gain = jnp.where(jnp.arange(MAXSTEP)[:, None] < step_counts[None, :], 0.5 * step[None, :], 0.0)
    f32, bf16 = jnp.float32, jnp.bfloat16
    tall = 2 * dof + 8
    slabs = (xs, ny, dof, width)
    dma = pltpu.SemaphoreType.DMA
    result = pl.pallas_call(
        functools.partial(kernel, nt, nx, ny),
        out_shape=jax.ShapeDtypeStruct((ny, xs, dof, width), f32),
        in_specs=[pl.BlockSpec(memory_space=pltpu.VMEM)] * 2 + [pl.BlockSpec(memory_space=pltpu.SMEM)] * 2,
        out_specs=pl.BlockSpec(memory_space=pltpu.VMEM),
        scratch_shapes=[
            pltpu.VMEM((xs, ny, tall, width), f32),
            pltpu.VMEM((8 * dof, 3 * dof), bf16),
            pltpu.VMEM((xs + 2, ny, 8 * dof, width), f32),
            pltpu.VMEM(slabs, f32),
            pltpu.VMEM(slabs, f32),
            pltpu.VMEM(slabs, f32),
            pltpu.VMEM(slabs, f32),
            pltpu.VMEM((ny, xs, dof, width), f32),
            pltpu.VMEM((ny, xs, dof, width), f32),
            pltpu.VMEM((ny + 1, xs, dof, width), f32),
            pltpu.VMEM((2, 2, ny, dof, width), f32),
            pltpu.VMEM((max(1, ITERS * (nt - 1)), xs, dof, width), f32),
            pltpu.VMEM((ny * dof, 3 * dof), bf16),
            pltpu.VMEM((dof, 6 * dof), bf16),
            dma((3, xs)), dma((3, xs)),
            dma((2, 2, ny)), dma((2, 2, ny)),
            dma((xs, ny - 1)), dma((xs, ny - 1)),
            dma((xs, ny - 1)), dma((xs, ny - 1)),
            dma((max(1, ITERS * (nt - 1)), xs)), dma((max(1, ITERS * (nt - 1)), xs)),
        ],
        compiler_params=pltpu.CompilerParams(collective_id=0, has_side_effects=True, vmem_limit_bytes=50 << 20),
    )(mine, weights, step, gain)
    return result.reshape(ny, xs, dof, ys, ez).transpose(0, 2, 1, 3, 4)


def solution(mesh):
    nt, nx, ny = (mesh.shape[name] for name in ("tm", "gx", "gy"))
    return jax.shard_map(
        functools.partial(per_device, nt, nx, ny),
        mesh=mesh,
        in_specs=(
            P(None, "gx", "gy", None),
            P(None, "gx", "gy", None),
            P(),
            P(),
            P(),
            P("gx", "gy", None),
            P("tm"),
        ),
        out_specs=P("tm", None, "gx", "gy", None),
        check_vma=False,
    )
```

```python
import functools

import jax
import jax.numpy as jnp
from jax import lax
from jax.experimental import pallas as pl
from jax.experimental.pallas import tpu as pltpu
from jax.sharding import PartitionSpec as P

MAXSTEP = 3
ITERS = 2
MESH = pl.DeviceIdType.MESH


def split3(v):
    high = v.astype(jnp.bfloat16)
    low = (v - high.astype(jnp.float32)).astype(jnp.bfloat16)
    return jnp.concatenate([high, low, high], axis=0)


def split3_weights(w):
    high = w.astype(jnp.bfloat16)
    low = (w - high.astype(jnp.float32)).astype(jnp.bfloat16)
    return jnp.concatenate([high, high, low], axis=1)


def mul(w, v3):
    return jnp.dot(w, v3, preferred_element_type=jnp.float32)


def kernel(nt, nx, ny, mine, weights, step_ref, gain_ref, out,
           field, wide, prod, cur, mid, slope, corr, recv, local, starts, halo, arrived, powers, mixer,
           gsend, grecv, hsend, hrecv, asend, arecv, bsend, brecv, tsend, trecv):
    tm, gx, gy = lax.axis_index("tm"), lax.axis_index("gx"), lax.axis_index("gy")
    right, left = lax.rem(gx + 1, nx), lax.rem(gx + nx - 1, nx)
    later, earlier = lax.rem(tm + 1, nt), lax.rem(tm + nt - 1, nt)
    sibling = gy + 1 - 2 * lax.rem(gy, 2)
    across, beyond = ny - 1 - gy, ny - 1 - sibling
    peers = [across, beyond, sibling]
    xs = mine.shape[0]
    dof = weights.shape[1]
    edges, inside = [0, xs - 1], list(range(1, xs - 1))

    barrier = pltpu.get_barrier_semaphore()
    for target in [{"gx": left}, {"gx": right}, {"tm": later}, {"tm": earlier}] + [{"gy": p} for p in peers]:
        pl.semaphore_signal(barrier, inc=1, device_id=target, device_id_type=MESH)
    pl.semaphore_wait(barrier, 4 + len(peers))

    def remote(source, target, send, receive, device):
        return pltpu.make_async_remote_copy(src_ref=source, dst_ref=target, send_sem=send, recv_sem=receive,
                                            device_id=device, device_id_type=MESH)

    def halo_copies(slot, y):
        source = mid if slot == 1 else cur
        return [
            remote(source.at[0, y], halo.at[slot, 1, y], hsend.at[slot, 0, y], hrecv.at[slot, 1, y], {"gx": left}),
            remote(source.at[xs - 1, y], halo.at[slot, 0, y], hsend.at[slot, 1, y], hrecv.at[slot, 0, y], {"gx": right}),
        ]

    def send_halo(slot, y):
        for copy in halo_copies(slot, y):
            copy.start()

    crossing, passing, onward = {}, {}, {}
    for x in edges + inside:
        crossing[x] = remote(mine.at[x], field.at[x, gy], gsend.at[0, x], grecv.at[0, x], {"gy": across})
        passing[x] = remote(mine.at[x], field.at[x, gy], gsend.at[1, x], grecv.at[1, x], {"gy": sibling})
        onward[x] = remote(field.at[x, across], field.at[x, across], gsend.at[2, x], grecv.at[2, x], {"gy": sibling})
        crossing[x].start()
        passing[x].start()

    wide[...] = split3_weights(weights[...])
    coarse = wide[7 * dof:8 * dof, :]
    power = weights[7 * dof:8 * dof, :]
    for j in range(ny):
        powers[j * dof:(j + 1) * dof, :] = split3_weights(power)
        power = mul(coarse, split3(power)) if j < ny - 1 else power
    rows = lax.broadcasted_iota(jnp.int32, (dof, dof), 0)
    cols = lax.broadcasted_iota(jnp.int32, (dof, dof), 1)
    identity = (rows == cols).astype(jnp.float32)

    def raise_power(_, pair):
        high, total = pair
        return mul(coarse, split3(high)), mul(coarse, split3(total)) + identity

    high, total = lax.fori_loop(0, tm * ny + gy, raise_power, (identity, jnp.zeros_like(identity)))
    mixer[...] = jnp.concatenate([split3_weights(high), split3_weights(total)], axis=1)
    for x in edges + inside:
        field[x, gy] = mine[x]
        crossing[x].wait()
        onward[x].start()
        passing[x].wait()
        onward[x].wait()
        for y in range(ny):
            cur[x, y] = mul(mixer[...], jnp.concatenate(
                [split3(field[x, y, 0:dof, :]), split3(field[x, y, dof:2 * dof, :])], axis=0))
        if x == edges[-1]:
            for y in peers + [gy]:
                send_halo(0, y)

    step = step_ref[gy]

    def combine(x, y):
        here = prod.at[x + 1, y]

        def mask(f):
            return field[x, y, 2 * dof + f:2 * dof + f + 1, :]

        lower, upper = prod.at[x + 1, lax.rem(y + ny - 1, ny)], prod.at[x + 1, lax.rem(y + 1, ny)]

        def face(f):
            return slice((f + 1) * dof, (f + 2) * dof)

        before = jnp.concatenate([lower[face(2), 128:], here[face(2), :128]], axis=1)
        after = jnp.concatenate([here[face(3), 128:], upper[face(3), :128]], axis=1)
        below = jnp.concatenate([pltpu.roll(here[face(4), :128], 1, 1), pltpu.roll(here[face(4), 128:], 1, 1)], axis=1)
        above = jnp.concatenate([pltpu.roll(here[face(5), :128], 127, 1), pltpu.roll(here[face(5), 128:], 127, 1)], axis=1)
        total = here[0:dof, :] + field[x, y, dof:2 * dof, :]
        total = total + mask(0) * prod[x, y, face(0), :]
        total = total + mask(1) * prod[x + 2, y, face(1), :]
        total = total + mask(2) * before
        total = total + mask(3) * after
        total = total + mask(4) * below
        return total + mask(5) * above

    def stage(slot, finish, after_inside, after_edge):
        source = mid if slot == 1 else cur

        def products(x, _):
            for y in range(ny):
                prod[x + 1, y] = mul(wide[...], split3(source[x, y]))
            return 0

        lax.fori_loop(0, xs, products, 0)

        def inner(x, _):
            for y in range(ny):
                finish(x, y, combine(x, y))
            return 0

        lax.fori_loop(1, xs - 1, inner, 0)
        after_inside()
        for y in peers + [gy]:
            for copy in halo_copies(slot, y):
                copy.wait()
            prod[0, y, dof:2 * dof, :] = mul(wide[dof:2 * dof, :], split3(halo[slot, 0, y]))
            prod[xs + 1, y, 2 * dof:3 * dof, :] = mul(wide[2 * dof:3 * dof, :], split3(halo[slot, 1, y]))
            for x in edges:
                finish(x, y, combine(x, y))
            after_edge(y)

    def nothing(*_):
        return None

    def to_middle(x, y, rate):
        slope[x, y] = rate
        mid[x, y] = cur[x, y] + step * rate

    def advance(number, _):
        gain = gain_ref[number, gy]

        def to_next(x, y, rate):
            cur[x, y] = cur[x, y] + gain * (slope[x, y] + rate)

        stage(0, to_middle, nothing, functools.partial(send_halo, 1))
        stage(1, to_next, nothing, functools.partial(send_halo, 0))
        return 0

    def incoming(at, x):
        return jnp.where(tm == 0, mine[x, 0:dof, :], arrived[at, x])

    for iteration in range(ITERS):
        last = iteration == ITERS - 1

        def keep_coarse(x, _):
            for y in range(ny):
                corr[x, y] = mul(coarse, split3(cur[x, y]))
            return 0

        lax.fori_loop(0, xs, keep_coarse, 0)
        lax.fori_loop(0, MAXSTEP - 1, advance, 0)
        gain = gain_ref[MAXSTEP - 1, gy]
        giving = {}

        def to_correction(x, y, rate):
            corr[x, y] = cur[x, y] + gain * (slope[x, y] + rate) - corr[x, y]

        for x in range(xs):
            for d, peer in enumerate(peers):
                giving[x, d] = remote(corr.at[x, peer], recv.at[gy, x], asend.at[x, d], arecv.at[x, d], {"gy": peer})

        def give(places, reached):
            for x in places:
                for d, peer in enumerate(peers):
                    if any(peer is y for y in reached):
                        giving[x, d].start()

        def give_edge(y):
            give(edges, [y])

        stage(0, to_middle, nothing, functools.partial(send_halo, 1))
        stage(1, to_correction, functools.partial(give, inside, peers), give_edge)

        relays = {}

        def relay(number, x, entering):
            at = iteration * (nt - 1) + number
            starts[ny, x] = mul(powers[(ny - 1) * dof:, :], split3(entering)) + local[ny - 1, x]
            relays[x] = remote(starts.at[ny, x], arrived.at[at, x], tsend.at[at, x], trecv.at[at, x], {"tm": later})
            relays[x].start()

        taking = {}

        def sweep_from_zero(x):
            recv[gy, x] = corr[x, gy]
            for d in range(len(peers)):
                giving[x, d].wait()
            now = recv[0, x]
            local[0, x] = now
            for j in range(1, ny):
                now = mul(coarse, split3(now)) + recv[j, x]
                local[j, x] = now
            if nt > 1:
                relay(0, x, mine[x, 0:dof, :])

        def sweep_on(x):
            if nt > 1:
                relays[x].wait()
                starts[0, x] = incoming(iteration * (nt - 1) + nt - 2, x)
            else:
                starts[0, x] = mine[x, 0:dof, :]
            shares = mul(powers[...], split3(starts[0, x]))
            for j in range(ny):
                ended = shares[j * dof:(j + 1) * dof, :] + local[j, x]
                if last:
                    out[j, x] = ended
                elif j < ny - 1:
                    starts[j + 1, x] = ended
            if not last:
                cur[x, gy] = starts[gy, x]
                for d, peer in enumerate(peers):
                    taking[x, d] = remote(starts.at[peer, x], cur.at[x, gy], bsend.at[x, d], brecv.at[x, d], {"gy": peer})
                    taking[x, d].start()

        for places in (inside, edges):
            for x in places:
                sweep_from_zero(x)
            for number in range(1, nt - 1):
                for x in places:
                    relays[x].wait()
                    relay(number, x, incoming(iteration * (nt - 1) + number - 1, x))
            for x in places:
                sweep_on(x)
        if not last:
            send_halo(0, gy)
            for d in range(len(peers)):
                for x in edges:
                    taking[x, d].wait()
                send_halo(0, peers[d])
            for x in inside:
                for d in range(len(peers)):
                    taking[x, d].wait()


def per_device(nt, nx, ny, initial, source, self_block, face_blocks, coarse_block, face_code, step_counts):
    dof, xs, ys, ez = initial.shape
    assert step_counts.shape[0] == ny == 4
    width = ys * ez
    depth = jnp.arange(ez)
    powers = (2 ** jnp.arange(6)).astype(jnp.int32)
    faces = (face_code[:, None] // powers[None, :, None, None] % 2).astype(jnp.float32)
    inside = jnp.ones((6, ez), jnp.float32).at[4].set((depth > 0) * 1.0).at[5].set((depth < ez - 1) * 1.0)
    faces = faces * inside[None, :, None, :]
    faces = jnp.pad(faces, ((0, 0), (0, 2), (0, 0), (0, 0))).reshape(xs, 8, width)

    def chunked(v):
        return v.transpose(1, 0, 2, 3).reshape(xs, dof, width)

    mine = jnp.concatenate([chunked(initial), chunked(source), faces], axis=1)
    weights = jnp.concatenate([self_block[None], face_blocks, coarse_block[None]], axis=0).reshape(8 * dof, dof)
    step = 1.0 / step_counts.astype(jnp.float32)
    gain = jnp.where(jnp.arange(MAXSTEP)[:, None] < step_counts[None, :], 0.5 * step[None, :], 0.0)
    f32, bf16 = jnp.float32, jnp.bfloat16
    tall = 2 * dof + 8
    slabs = (xs, ny, dof, width)
    dma = pltpu.SemaphoreType.DMA
    result = pl.pallas_call(
        functools.partial(kernel, nt, nx, ny),
        out_shape=jax.ShapeDtypeStruct((ny, xs, dof, width), f32),
        in_specs=[pl.BlockSpec(memory_space=pltpu.VMEM)] * 2 + [pl.BlockSpec(memory_space=pltpu.SMEM)] * 2,
        out_specs=pl.BlockSpec(memory_space=pltpu.VMEM),
        scratch_shapes=[
            pltpu.VMEM((xs, ny, tall, width), f32),
            pltpu.VMEM((8 * dof, 3 * dof), bf16),
            pltpu.VMEM((xs + 2, ny, 8 * dof, width), f32),
            pltpu.VMEM(slabs, f32),
            pltpu.VMEM(slabs, f32),
            pltpu.VMEM(slabs, f32),
            pltpu.VMEM(slabs, f32),
            pltpu.VMEM((ny, xs, dof, width), f32),
            pltpu.VMEM((ny, xs, dof, width), f32),
            pltpu.VMEM((ny + 1, xs, dof, width), f32),
            pltpu.VMEM((2, 2, ny, dof, width), f32),
            pltpu.VMEM((max(1, ITERS * (nt - 1)), xs, dof, width), f32),
            pltpu.VMEM((ny * dof, 3 * dof), bf16),
            pltpu.VMEM((dof, 6 * dof), bf16),
            dma((3, xs)), dma((3, xs)),
            dma((2, 2, ny)), dma((2, 2, ny)),
            dma((xs, ny - 1)), dma((xs, ny - 1)),
            dma((xs, ny - 1)), dma((xs, ny - 1)),
            dma((max(1, ITERS * (nt - 1)), xs)), dma((max(1, ITERS * (nt - 1)), xs)),
        ],
        compiler_params=pltpu.CompilerParams(collective_id=0, has_side_effects=True, vmem_limit_bytes=50 << 20),
    )(mine, weights, step, gain)
    return result.reshape(ny, xs, dof, ys, ez).transpose(0, 2, 1, 3, 4)


def solution(mesh):
    nt, nx, ny = (mesh.shape[name] for name in ("tm", "gx", "gy"))
    return jax.shard_map(
        functools.partial(per_device, nt, nx, ny),
        mesh=mesh,
        in_specs=(
            P(None, "gx", "gy", None),
            P(None, "gx", "gy", None),
            P(),
            P(),
            P(),
            P("gx", "gy", None),
            P("tm"),
        ),
        out_specs=P("tm", None, "gx", "gy", None),
        check_vma=False,
    )
```
